512 devices in a mesh: chan: 128 (over z, x, y_lo), rep: 4 (over y_hi, core).
Axes of the slice: x: 4, y: 8 (y_hi: 2, y_lo: 4; y = y_hi * 4 + y_lo), z: 8, core: 2. Of those that a mesh axis runs over, the one named last changes fastest.
Arguments:
- strain: bfloat16 [2048, 131072], P('chan', 'rep'), may hold values from -60 to 60
- fir_taps: float32 [60], replicated, may hold values from -0.75 to 0.75
- spatial: float32 [9], replicated, may hold values from -2 to 2
Outputs:
- cross_tiles: float32 [2048, 5, 32, 32], P('chan', None, 'rep')
The draws below stay inside these ranges and needn't reach their ends.
All inputs are finite; a program needn't handle non-finite values.
Results may differ from the reference program's by a relative error of at most 0.0023.
Values may be sent and summed in bfloat16 or wider, within the bound.
A program may use at most 64 MiB of HBM per device.

```python
import math
import jax
import jax.numpy as jnp
from jax import lax

CB = 16
TAPS = 60
SPAN = 9
NFFT = 1024
BINS = 32
FIRST_BIN = 16
BLOCKS = 128
CHANNELS = 2048
WINDOWS = 128
SAMPLES = 131072
OFFSETS = 5


def draw_strain(key, part):
    noise_key = jax.random.fold_in(key, 11)
    level_key = jax.random.fold_in(key, 23)
    window_count = SAMPLES // NFFT
    raw_noise = jnp.clip(jax.random.normal(noise_key, (CHANNELS, window_count, NFFT), jnp.float32), -6.0, 6.0)
    level_grid = jnp.exp(jax.random.uniform(level_key, (CHANNELS, window_count, 1), jnp.float32, 0.0, jnp.log(10.0)))
    return (raw_noise * level_grid).reshape(CHANNELS, SAMPLES).astype(jnp.bfloat16)


def centred(own_key, dims, scale, limit, kind=jnp.bfloat16):
    entries = jax.random.normal(own_key, dims, jnp.float32) * scale
    return jnp.minimum(jnp.maximum(entries, -limit), limit).astype(kind)


def setup_inputs(seed: int = 0) -> dict:
    seeds = jax.random.split(jax.random.key(seed), 4)
    return {
        "strain": draw_strain(jax.random.fold_in(seeds[3], 71), 0),
        "fir_taps": centred(seeds[1], (TAPS,), TAPS ** -0.5, 0.75, jnp.float32),
        "spatial": centred(seeds[2], (SPAN,), SPAN ** -0.5, 2.0, jnp.float32),
    }


epsilon = 1e-05

def toeplitz_pair(fir_taps):
    source_pos = jnp.arange(128, dtype=jnp.int32)[:, None]
    target_pos = jnp.arange(128, dtype=jnp.int32)[None, :]
    tap_slots = jnp.arange(fir_taps.shape[0], dtype=jnp.int32)
    lag_now = (target_pos - source_pos)[:, :, None]
    lag_before = (target_pos + 128 - source_pos)[:, :, None]
    zero_value = jnp.zeros((), fir_taps.dtype)
    taps_now = lax.optimization_barrier(jnp.sum(jnp.where(lag_now == tap_slots, fir_taps, zero_value), axis=2))
    taps_before = lax.optimization_barrier(jnp.sum(jnp.where(lag_before == tap_slots, fir_taps, zero_value), axis=2))
    return (taps_now, taps_before)

def dft_table(bin_count, first_bin, dft_length, float_type):
    sample_pos = jnp.arange(dft_length, dtype=jnp.int32)[:, None]
    freq_bins = (first_bin + jnp.arange(bin_count, dtype=jnp.int32))[None, :]
    phase_index = sample_pos * freq_bins % dft_length
    phase_angle = phase_index.astype(float_type) * (2.0 * math.pi / dft_length)
    inverse_root = 1.0 / math.sqrt(dft_length)
    return jnp.concatenate([jnp.cos(phase_angle), -jnp.sin(phase_angle)], axis=1) * inverse_root

def window_spectra(channel_rows, spatial, taps_now, taps_before, dft_matrix):
    filter_span = spatial.shape[0]
    row_count = channel_rows.shape[0] - filter_span + 1
    mixed_rows = spatial[0] * channel_rows[0:row_count]
    for offset in range(1, filter_span):
        mixed_rows = mixed_rows + spatial[offset] * channel_rows[offset:offset + row_count]
    time_blocks = mixed_rows.reshape(row_count, -1, 128)
    band_pass = jnp.einsum('cbj,ji->cbi', time_blocks[:, 1:], taps_now, precision=lax.Precision.HIGHEST)
    band_pass = band_pass + jnp.einsum('cbj,ji->cbi', time_blocks[:, :-1], taps_before, precision=lax.Precision.HIGHEST)
    window_data = band_pass.reshape(row_count, -1, dft_matrix.shape[0])
    window_power = lax.optimization_barrier(jnp.mean(window_data * window_data, axis=2, keepdims=True))
    normalized = window_data / jnp.sqrt(window_power + epsilon)
    spectra = jnp.einsum('cwn,nm->cwm', normalized, dft_matrix, precision=lax.Precision.HIGHEST)
    return spectra.reshape(row_count, spectra.shape[1], 2, -1).astype(jnp.bfloat16)

def cross_tile(own_spec, other_spec):
    own_real, own_imag = (own_spec[:, :, 0], own_spec[:, :, 1])
    other_real, other_imag = (other_spec[:, :, 0], other_spec[:, :, 1])
    cross_real = jnp.einsum('cwf,kwf->cfk', own_real, other_real, preferred_element_type=jnp.float32, precision=lax.Precision.HIGHEST)
    cross_real = cross_real + jnp.einsum('cwf,kwf->cfk', own_imag, other_imag, preferred_element_type=jnp.float32, precision=lax.Precision.HIGHEST)
    cross_imag = jnp.einsum('cwf,kwf->cfk', own_imag, other_real, preferred_element_type=jnp.float32, precision=lax.Precision.HIGHEST)
    cross_imag = cross_imag - jnp.einsum('cwf,kwf->cfk', own_real, other_imag, preferred_element_type=jnp.float32, precision=lax.Precision.HIGHEST)
    return jnp.concatenate([cross_real, cross_imag], axis=2)

def reference(strain, fir_taps, spatial):
    taps_now, taps_before = toeplitz_pair(fir_taps)
    dft_matrix = dft_table(BINS, FIRST_BIN, NFFT, fir_taps.dtype)
    rim_width = (SPAN - 1) // 2
    padded = jnp.pad(strain, ((rim_width, rim_width), (128, 0)))

    def one_block(block_index):
        channel_rows = lax.dynamic_slice_in_dim(padded, (block_index * CB).astype(jnp.int32), CB + 2 * rim_width, 0)
        return window_spectra(channel_rows.astype(jnp.float32), spatial, taps_now, taps_before, dft_matrix)
    spectra = lax.map(one_block, jnp.arange(BLOCKS, dtype=jnp.int32))
    inverse = 1.0 / WINDOWS

    def one_tile_row(block_index):
        own_spec = spectra[block_index].astype(jnp.float32)
        tile_list = []
        for offset in range(OFFSETS):
            partner = spectra[(block_index + offset) % BLOCKS].astype(jnp.float32)
            tile_list.append(cross_tile(own_spec, partner))
        return jnp.stack(tile_list, axis=1) * inverse
    cross_tiles = lax.map(one_tile_row, jnp.arange(BLOCKS, dtype=jnp.int32))
    return cross_tiles.reshape(CHANNELS, OFFSETS, BINS, 2 * CB)
```

```python
import functools
import math

import jax
import jax.numpy as jnp
import ml_dtypes
import numpy as np
from jax import lax
from jax.experimental import pallas as pl
from jax.experimental.pallas import tpu as pltpu
from jax.sharding import PartitionSpec as P

NFFT = 1024
BINS = 32
FIRST_BIN = 16
EPSILON = 1e-05
LANES = 128
CW = 8
GROUP = 8
BLOCKS_PER_WINDOW = NFFT // LANES
MESH = pl.DeviceIdType.MESH
F32 = jnp.float32
BF16 = jnp.bfloat16


def split_table(values):
    high = values.astype(ml_dtypes.bfloat16)
    low = (values - high.astype(np.float64)).astype(ml_dtypes.bfloat16)
    return high, low


def tables():
    sample = np.arange(LANES)[:, None, None]
    block = np.arange(BLOCKS_PER_WINDOW)[None, :, None]
    bins = (FIRST_BIN + np.arange(BINS))[None, None, :]
    angle = ((block * LANES + sample) * bins % NFFT) * (2.0 * math.pi / NFFT)
    parts = np.concatenate([np.cos(angle), -np.sin(angle)], axis=2) / math.sqrt(NFFT)
    parts = np.concatenate([parts, np.zeros_like(parts)], axis=2)
    high, low = split_table(parts.reshape(LANES, BLOCKS_PER_WINDOW * LANES))
    row = np.arange(2 * BINS)[:, None]
    lane = np.arange(1024)[None, :]
    source = (lane // 512) * BINS + (lane % 512) // LANES * GROUP + lane % GROUP
    choose = (row == source).astype(ml_dtypes.bfloat16)
    return np.concatenate([high, low, choose], axis=0)


def iota(shape, dim):
    return lax.broadcasted_iota(jnp.int32, shape, dim)


def dot(a, b):
    return jnp.dot(a, b, preferred_element_type=F32)


def kernel(
    chans, reps, strain, taps, spatial, table, out,
    own, rim, fir_w, fold_w, tab, filt, raw, power_low, own_raw, packs, gathered, tiles,
    local_sem, rim_send, rim_recv, hist_send, hist_recv, one_send, one_recv, two_send, two_recv,
):
    b = lax.axis_index("chan")
    r = lax.axis_index("rep")
    samples = strain.shape[1]
    windows = samples // NFFT
    chunks = windows // CW
    span = CW * NFFT

    def block_at(step):
        return lax.rem(b + (step + chans), chans)

    def rep_at(step):
        return lax.rem(r + (step + reps), reps)

    barrier = pltpu.get_barrier_semaphore()
    peers = [(s, 0) for s in (-4, -3, -2, -1, 1, 2, 3, 4)] + [(0, d) for d in range(1, reps)] + [(-1, 1), (1, -1)]
    for s, d in peers:
        pl.semaphore_signal(
            barrier, inc=1, device_id={"chan": block_at(s), "rep": rep_at(d)}, device_id_type=MESH
        )
    fetch_own = pltpu.make_async_copy(strain, own.at[:, pl.ds(LANES, samples)], local_sem.at[0])
    fetch_own.start()
    fetch_tab = pltpu.make_async_copy(table, tab, local_sem.at[1])
    fetch_tab.start()

    row, lane = iota((LANES, LANES), 0), iota((LANES, LANES), 1)
    tap_row = jnp.concatenate([taps[...], jnp.zeros((1, LANES - taps.shape[1]), F32)], axis=1)
    circulant = pltpu.roll(jnp.broadcast_to(tap_row, (LANES, LANES)), 0, 1, stride=1, stride_axis=0)
    now = jnp.where(lane >= row, circulant, 0.0)
    before = jnp.where(lane < row, circulant, 0.0)
    both = jnp.concatenate([before, now], axis=0)
    both_high = both.astype(BF16)
    both_low = (both - both_high.astype(F32)).astype(BF16)
    fir_w[:, 0:LANES] = both_high
    fir_w[:, LANES:] = both_low
    fetch_tab.wait()
    folded = dot(
        jnp.concatenate([both_high, both_low, both_high], axis=1),
        jnp.concatenate([tab[0:LANES], tab[0:LANES], tab[LANES : 2 * LANES]], axis=0),
    )
    for q in range(BLOCKS_PER_WINDOW + 1):
        part = jnp.zeros((LANES, LANES), F32)
        if q > 0:
            part = part + folded[LANES:, (q - 1) * LANES : q * LANES]
        if q < BLOCKS_PER_WINDOW:
            part = part + folded[0:LANES, q * LANES : (q + 1) * LANES]
        part_high = part.astype(BF16)
        fold_w[q * LANES : (q + 1) * LANES, 0:LANES] = part_high
        fold_w[q * LANES : (q + 1) * LANES, LANES:] = (part - part_high.astype(F32)).astype(BF16)

    half_row = iota((8, LANES), 0)
    weights = [spatial[j] for j in range(9)]
    crossing = []
    for j in range(9):
        same = (half_row < 4) == (half_row + (8 + j) < 16)
        keep = jnp.logical_or(same, b != chans - 1)
        crossing.append(jnp.where(keep, weights[j], 0.0))

    pl.semaphore_wait(barrier, len(peers))

    rim_copies = []
    for k in range(chunks):
        if k == 0:
            source = strain.at[pl.ds(0, 8), pl.ds(0, span)]
            target = rim.at[k, :, pl.ds(LANES, span)]
        else:
            source = strain.at[pl.ds(0, 8), pl.ds(k * span - LANES, span + LANES)]
            target = rim.at[k]
        rim_copies.append(
            pltpu.make_async_remote_copy(
                source, target, rim_send.at[k], rim_recv.at[k],
                device_id={"chan": block_at(-1), "rep": r}, device_id_type=MESH,
            )
        )
    hist_own = pltpu.make_async_remote_copy(
        strain.at[:, pl.ds(samples - LANES, LANES)], own.at[:, pl.ds(0, LANES)],
        hist_send.at[0], hist_recv.at[0],
        device_id={"chan": b, "rep": rep_at(1)}, device_id_type=MESH,
    )
    hist_rim = pltpu.make_async_remote_copy(
        strain.at[pl.ds(0, 8), pl.ds(samples - LANES, LANES)], rim.at[0, :, pl.ds(0, LANES)],
        hist_send.at[1], hist_recv.at[1],
        device_id={"chan": block_at(-1), "rep": rep_at(1)}, device_id_type=MESH,
    )
    hist_own.start()
    hist_rim.start()
    for k in reversed(range(chunks)):
        rim_copies[k].start()
    fetch_own.wait()

    def lower_window(w):
        base = pl.multiple_of(w * NFFT, LANES)
        left = jnp.concatenate([own[:, pl.ds(base + i * LANES, 2 * LANES)] for i in range(BLOCKS_PER_WINDOW)], axis=0)
        both_parts = dot(left, fir_w[...])
        band = both_parts[:, 0:LANES] + both_parts[:, LANES:]
        for i in range(BLOCKS_PER_WINDOW):
            filt[w, i * 24 : i * 24 + 16, :] = band[i * 16 : i * 16 + 16]
        squares = jnp.zeros((8, LANES), F32)
        for i in range(BLOCKS_PER_WINDOW):
            mixed = weights[0] * filt[w, i * 24 : i * 24 + 8, :]
            for j in range(1, 9):
                mixed = mixed + weights[j] * filt[w, i * 24 + j : i * 24 + j + 8, :]
            squares = squares + mixed * mixed
        power_low[w] = squares

    def lower_chunk(k):
        first = k * CW

        def body(t, carry):
            lower_window(first + t)
            return carry

        lax.fori_loop(0, CW, body, 0)
        left = jnp.concatenate(
            [own[:, pl.ds((first + t) * NFFT, NFFT + LANES)] for t in range(CW)], axis=0
        )
        parts = dot(left, fold_w[...])
        own_raw[k] = parts[:, 0:LANES] + parts[:, LANES:]

    def upper_chunk(k):
        first = k * CW

        def body(t, carry):
            w = first + t
            base = pl.multiple_of(t * NFFT, LANES)
            left = jnp.concatenate(
                [rim[k, :, pl.ds(base + i * LANES, 2 * LANES)] for i in range(BLOCKS_PER_WINDOW)], axis=0
            )
            both_parts = dot(left, fir_w[...])
            band = both_parts[:, 0:LANES] + both_parts[:, LANES:]
            for i in range(BLOCKS_PER_WINDOW):
                filt[w, i * 24 + 16 : i * 24 + 24, :] = band[i * 8 : i * 8 + 8]
            squares = jnp.zeros((8, LANES), F32)
            for i in range(BLOCKS_PER_WINDOW):
                mixed = crossing[0] * filt[w, i * 24 + 8 : i * 24 + 16, :]
                for j in range(1, 9):
                    mixed = mixed + crossing[j] * filt[w, i * 24 + 8 + j : i * 24 + 16 + j, :]
                squares = squares + mixed * mixed
            raw[t, 24:32, :] = squares
            return carry

        lax.fori_loop(0, CW, body, 0)
        left = jnp.concatenate([rim[k, :, pl.ds(t * NFFT, NFFT + LANES)] for t in range(CW)], axis=0)
        parts = dot(left, fold_w[...])
        rim_raw = parts[:, 0:LANES] + parts[:, LANES:]
        pieces = []
        for t in range(CW):
            raw[t, 0:16, :] = own_raw[k, t * 16 : t * 16 + 16, :]
            raw[t, 16:24, :] = rim_raw[t * 8 : t * 8 + 8]
            lower = weights[0] * raw[t, 0:8, :]
            upper = crossing[0] * raw[t, 8:16, :]
            for j in range(1, 9):
                lower = lower + weights[j] * raw[t, j : j + 8, :]
                upper = upper + crossing[j] * raw[t, 8 + j : 16 + j, :]
            for value, squares in ((lower, power_low[first + t]), (upper, raw[t, 24:32, :])):
                mean = jnp.sum(squares, axis=1, keepdims=True) * (1.0 / NFFT)
                pieces.append(value / jnp.sqrt(mean + EPSILON))
        spectra = jnp.concatenate(pieces, axis=0).astype(BF16)
        spread = dot(spectra[:, 0 : 2 * BINS], tab[2 * LANES : 2 * LANES + 2 * BINS])
        rows, lanes = iota((LANES, LANES), 0), iota((LANES, LANES), 1)
        mine = lax.rem(lax.rem(rows, 16) + 4, 16) == lanes // GROUP
        columns = [
            jnp.where(mine, spread[:, g * LANES : (g + 1) * LANES], 0.0).astype(BF16) for g in range(8)
        ]
        stacked = jnp.concatenate(
            [jnp.concatenate(columns[0:4], axis=1), jnp.concatenate(columns[4:8], axis=1)], axis=0
        )
        collect = jnp.where(
            iota((16, 256), 0) == iota((16, 256), 1) // 16, 1.0, 0.0
        ).astype(BF16)
        packed = dot(collect, stacked).astype(BF16)
        for g in range(reps):
            packs[k, g] = packed[:, g * LANES : (g + 1) * LANES]
        gathered[1, k, r] = packs[k, r]

    def first_copy(k, d):
        return pltpu.make_async_remote_copy(
            packs.at[k, rep_at(d)], gathered.at[1, k, r], one_send.at[k, d - 1], one_recv.at[k, d - 1],
            device_id={"chan": b, "rep": rep_at(d)}, device_id_type=MESH,
        )

    def second_copy(k, s):
        slot = 0 if s == 0 else s + 1
        return pltpu.make_async_remote_copy(
            gathered.at[1, k], gathered.at[slot, k], two_send.at[k, s], two_recv.at[k, s],
            device_id={"chan": block_at(1 if s == 0 else -s), "rep": r}, device_id_type=MESH,
        )

    order = list(reversed(range(chunks)))
    for k in order:
        if k == 0:
            hist_own.wait_recv()

            @pl.when(r == 0)
            def _():
                own[:, 0:LANES] = jnp.zeros((16, LANES), BF16)

        lower_chunk(k)

    def forward(k):
        for d in range(1, reps):
            first_copy(k, d).wait_recv()
        for s in range(5):
            second_copy(k, s).start()

    for place, k in enumerate(order):
        rim_copies[k].wait_recv()
        if k == 0:
            hist_rim.wait_recv()

            @pl.when(r == 0)
            def _():
                rim[0, :, 0:LANES] = jnp.zeros((8, LANES), BF16)

        upper_chunk(k)
        for d in range(1, reps):
            first_copy(k, d).start()
        if place > 0:
            forward(order[place - 1])
    forward(order[-1])
    for k in order:
        for s in range(5):
            second_copy(k, s).wait_recv()

    depth = chunks * reps * 16
    own_lanes = iota((depth, LANES), 1) < 32

    def merged(s):
        return jnp.where(
            own_lanes,
            gathered[s].reshape(depth, LANES).astype(F32),
            gathered[s + 1].reshape(depth, LANES).astype(F32),
        )

    mine = merged(0)
    cubes = mine.reshape(chunks * reps, 2, 8, LANES)
    swapped = jnp.concatenate([cubes[:, 1:2], -cubes[:, 0:1]], axis=1).reshape(depth, LANES)
    left = jnp.concatenate([mine.T, swapped.T], axis=0).astype(BF16)
    same_bin = lax.rem(iota((LANES, LANES), 0), GROUP) == lax.rem(iota((LANES, LANES), 1), GROUP)
    pick_row, pick_lane = iota((LANES, LANES), 0), iota((LANES, LANES), 1)
    pick_real = jnp.where(pick_lane == pick_row // GROUP, 1.0, 0.0).astype(BF16)
    pick_imag = jnp.where(pick_lane == 16 + pick_row // GROUP, 1.0, 0.0).astype(BF16)
    picks = jnp.concatenate([pick_real, pick_imag] * 3, axis=0)
    scale = 1.0 / (windows * reps)
    for s in range(5):
        block = (mine if s == 0 else merged(s)).astype(BF16)
        product = dot(left, block)
        real = jnp.where(same_bin, product[0:LANES], 0.0) * scale
        imag = jnp.where(same_bin, product[LANES:], 0.0) * scale
        terms = []
        for _ in range(3):
            real_part, imag_part = real.astype(BF16), imag.astype(BF16)
            terms += [real_part, imag_part]
            real, imag = real - real_part.astype(F32), imag - imag_part.astype(F32)
        tile = dot(jnp.concatenate(terms, axis=1), picks)
        for c in range(16):
            out[c, s] = tile[c * GROUP : (c + 1) * GROUP, 0:32]

    for k in range(chunks):
        rim_copies[k].wait_send()
        for d in range(1, reps):
            first_copy(k, d).wait_send()
        for s in range(5):
            second_copy(k, s).wait_send()
    hist_own.wait_send()
    hist_rim.wait_send()


def solution(mesh):
    chans, reps = mesh.shape["chan"], mesh.shape["rep"]

    def per_device(strain, fir_taps, spatial):
        rows, samples = strain.shape
        windows = samples // NFFT
        chunks = windows // CW
        span = CW * NFFT
        anywhere = pl.BlockSpec(memory_space=pl.ANY)
        vmem = pl.BlockSpec(memory_space=pltpu.VMEM)
        return pl.pallas_call(
            functools.partial(kernel, chans, reps),
            out_shape=jax.ShapeDtypeStruct((rows, 5, BINS // reps, 32), F32),
            in_specs=[anywhere, vmem, pl.BlockSpec(memory_space=pltpu.SMEM), anywhere],
            out_specs=vmem,
            scratch_shapes=[
                pltpu.VMEM((rows, samples + LANES), BF16),
                pltpu.VMEM((chunks, 8, span + LANES), BF16),
                pltpu.VMEM((2 * LANES, 2 * LANES), BF16),
                pltpu.VMEM((NFFT + LANES, 2 * LANES), BF16),
                pltpu.VMEM((2 * LANES + 2 * BINS, 1024), BF16),
                pltpu.VMEM((windows, 192, LANES), F32),
                pltpu.VMEM((CW, 32, LANES), F32),
                pltpu.VMEM((windows, 8, LANES), F32),
                pltpu.VMEM((chunks, CW * 16, LANES), F32),
                pltpu.VMEM((chunks, reps, 16, LANES), BF16),
                pltpu.VMEM((6, chunks, reps, 16, LANES), BF16),
                pltpu.VMEM((8, LANES), F32),
                pltpu.SemaphoreType.DMA((2,)),
                pltpu.SemaphoreType.DMA((chunks,)),
                pltpu.SemaphoreType.DMA((chunks,)),
                pltpu.SemaphoreType.DMA((2,)),
                pltpu.SemaphoreType.DMA((2,)),
                pltpu.SemaphoreType.DMA((chunks, 3)),
                pltpu.SemaphoreType.DMA((chunks, 3)),
                pltpu.SemaphoreType.DMA((chunks, 5)),
                pltpu.SemaphoreType.DMA((chunks, 5)),
            ],
            compiler_params=pltpu.CompilerParams(
                collective_id=0, has_side_effects=True, vmem_limit_bytes=40 * 1024 * 1024
            ),
        )(strain, fir_taps.reshape(1, -1), spatial, jnp.asarray(tables()))

    return jax.shard_map(
        per_device,
        mesh=mesh,
        in_specs=(P("chan", "rep"), P(), P()),
        out_specs=P("chan", None, "rep", None),
        check_vma=False,
    )
```

```python
import functools
import math

import jax
import jax.numpy as jnp
import ml_dtypes
import numpy as np
from jax import lax
from jax.experimental import pallas as pl
from jax.experimental.pallas import tpu as pltpu
from jax.sharding import PartitionSpec as P

NFFT = 1024
BINS = 32
FIRST_BIN = 16
EPSILON = 1e-05
LANES = 128
CW = 8
GROUP = 8
BLOCKS_PER_WINDOW = NFFT // LANES
MESH = pl.DeviceIdType.MESH
F32 = jnp.float32
BF16 = jnp.bfloat16


def split_table(values):
    high = values.astype(ml_dtypes.bfloat16)
    low = (values - high.astype(np.float64)).astype(ml_dtypes.bfloat16)
    return high, low


def tables():
    sample = np.arange(LANES)[:, None, None]
    block = np.arange(BLOCKS_PER_WINDOW)[None, :, None]
    bins = (FIRST_BIN + np.arange(BINS))[None, None, :]
    angle = ((block * LANES + sample) * bins % NFFT) * (2.0 * math.pi / NFFT)
    parts = np.concatenate([np.cos(angle), -np.sin(angle)], axis=2) / math.sqrt(NFFT)
    parts = np.concatenate([parts, np.zeros_like(parts)], axis=2)
    high, low = split_table(parts.reshape(LANES, BLOCKS_PER_WINDOW * LANES))
    row = np.arange(2 * BINS)[:, None]
    lane = np.arange(1024)[None, :]
    source = (lane // 512) * BINS + (lane % 512) // LANES * GROUP + lane % GROUP
    choose = (row == source).astype(ml_dtypes.bfloat16)
    return np.concatenate([high, low, choose], axis=0)


def iota(shape, dim):
    return lax.broadcasted_iota(jnp.int32, shape, dim)


def dot(a, b):
    return jnp.dot(a, b, preferred_element_type=F32)


def kernel(
    chans, reps, strain, taps_in, spatial_in, table, out,
    taps, spatial, own, rim, fir_w, fold_w, tab, filt, raw, power_low, own_raw, packs, gathered, tiles,
    local_sem, rim_send, rim_recv, hist_send, hist_recv, one_send, one_recv, two_send, two_recv,
):
    b = lax.axis_index("chan")
    r = lax.axis_index("rep")
    samples = strain.shape[1]
    windows = samples // NFFT
    chunks = windows // CW
    span = CW * NFFT

    def block_at(step):
        return lax.rem(b + (step + chans), chans)

    def rep_at(step):
        return lax.rem(r + (step + reps), reps)

    barrier = pltpu.get_barrier_semaphore()
    peers = [(s, 0) for s in (-4, -3, -2, -1, 1, 2, 3, 4)] + [(0, d) for d in range(1, reps)] + [(-1, 1), (1, -1)]
    for s, d in peers:
        pl.semaphore_signal(
            barrier, inc=1, device_id={"chan": block_at(s), "rep": rep_at(d)}, device_id_type=MESH
        )
    fetch_own = pltpu.make_async_copy(strain, own.at[:, pl.ds(LANES, samples)], local_sem.at[0])
    fetch_own.start()
    fetch_spatial = pltpu.make_async_copy(spatial_in, spatial, local_sem.at[2])
    fetch_spatial.start()
    fetch_taps = pltpu.make_async_copy(taps_in, taps, local_sem.at[3])
    fetch_taps.start()
    fetch_tab = pltpu.make_async_copy(table, tab, local_sem.at[1])
    fetch_tab.start()

    pl.semaphore_wait(barrier, len(peers))

    def rim_copy(k):
        return pltpu.make_async_remote_copy(
            strain.at[pl.ds(0, 8), pl.ds(k * span, span)],
            rim.at[:, pl.ds(pl.multiple_of(LANES + k * span, LANES), span)],
            rim_send.at[k], rim_recv.at[k],
            device_id={"chan": block_at(-1), "rep": r}, device_id_type=MESH,
        )

    hist_own = pltpu.make_async_remote_copy(
        strain.at[:, pl.ds(samples - LANES, LANES)], own.at[:, pl.ds(0, LANES)],
        hist_send.at[0], hist_recv.at[0],
        device_id={"chan": b, "rep": rep_at(1)}, device_id_type=MESH,
    )
    hist_rim = pltpu.make_async_remote_copy(
        strain.at[pl.ds(0, 8), pl.ds(samples - LANES, LANES)], rim.at[:, pl.ds(0, LANES)],
        hist_send.at[1], hist_recv.at[1],
        device_id={"chan": block_at(-1), "rep": rep_at(1)}, device_id_type=MESH,
    )
    hist_own.start()
    hist_rim.start()
    for k in range(chunks):
        rim_copy(k).start()

    row, lane = iota((LANES, LANES), 0), iota((LANES, LANES), 1)
    fetch_taps.wait()
    tap_row = jnp.concatenate([taps[...], jnp.zeros((1, LANES - taps.shape[1]), F32)], axis=1)
    circulant = pltpu.roll(jnp.broadcast_to(tap_row, (LANES, LANES)), 0, 1, stride=1, stride_axis=0)
    now = jnp.where(lane >= row, circulant, 0.0)
    before = jnp.where(lane < row, circulant, 0.0)
    both = jnp.concatenate([before, now], axis=0)
    both_high = both.astype(BF16)
    both_low = (both - both_high.astype(F32)).astype(BF16)
    fir_w[:, 0:LANES] = both_high
    fir_w[:, LANES:] = both_low
    fetch_tab.wait()
    folded = dot(
        jnp.concatenate([both_high, both_low, both_high], axis=1),
        jnp.concatenate([tab[0:LANES], tab[0:LANES], tab[LANES : 2 * LANES]], axis=0),
    )
    for q in range(BLOCKS_PER_WINDOW + 1):
        part = jnp.zeros((LANES, LANES), F32)
        if q > 0:
            part = part + folded[LANES:, (q - 1) * LANES : q * LANES]
        if q < BLOCKS_PER_WINDOW:
            part = part + folded[0:LANES, q * LANES : (q + 1) * LANES]
        part_high = part.astype(BF16)
        fold_w[q * LANES : (q + 1) * LANES, 0:LANES] = part_high
        fold_w[q * LANES : (q + 1) * LANES, LANES:] = (part - part_high.astype(F32)).astype(BF16)

    half_row = iota((8, LANES), 0)
    fetch_spatial.wait()
    weights = [spatial[j] for j in range(9)]
    crossing = []
    for j in range(9):
        same = (half_row < 4) == (half_row + (8 + j) < 16)
        keep = jnp.logical_or(same, b != chans - 1)
        crossing.append(jnp.where(keep, weights[j], 0.0))

    fetch_own.wait()

    def lower_window(w):
        base = pl.multiple_of(w * NFFT, LANES)
        left = jnp.concatenate([own[:, pl.ds(base + i * LANES, 2 * LANES)] for i in range(BLOCKS_PER_WINDOW)], axis=0)
        both_parts = dot(left, fir_w[...])
        band = both_parts[:, 0:LANES] + both_parts[:, LANES:]
        for i in range(BLOCKS_PER_WINDOW):
            filt[w, i * 24 : i * 24 + 16, :] = band[i * 16 : i * 16 + 16]
        squares = jnp.zeros((8, LANES), F32)
        for i in range(BLOCKS_PER_WINDOW):
            mixed = weights[0] * filt[w, i * 24 : i * 24 + 8, :]
            for j in range(1, 9):
                mixed = mixed + weights[j] * filt[w, i * 24 + j : i * 24 + j + 8, :]
            squares = squares + mixed * mixed
        power_low[w] = squares

    def lower_chunk(k):
        first = k * CW

        def body(t, carry):
            lower_window(first + t)
            return carry

        lax.fori_loop(0, CW, body, 0, unroll=2)
        left = jnp.concatenate(
            [own[:, pl.ds(pl.multiple_of((first + t) * NFFT, LANES), NFFT + LANES)] for t in range(CW)], axis=0
        )
        parts = dot(left, fold_w[...])
        own_raw[k] = parts[:, 0:LANES] + parts[:, LANES:]

    def upper_chunk(k):
        first = k * CW

        def body(t, carry):
            w = first + t
            base = pl.multiple_of(w * NFFT, LANES)
            left = jnp.concatenate(
                [rim[:, pl.ds(base + i * LANES, 2 * LANES)] for i in range(BLOCKS_PER_WINDOW)], axis=0
            )
            both_parts = dot(left, fir_w[...])
            band = both_parts[:, 0:LANES] + both_parts[:, LANES:]
            for i in range(BLOCKS_PER_WINDOW):
                filt[w, i * 24 + 16 : i * 24 + 24, :] = band[i * 8 : i * 8 + 8]
            squares = jnp.zeros((8, LANES), F32)
            for i in range(BLOCKS_PER_WINDOW):
                mixed = crossing[0] * filt[w, i * 24 + 8 : i * 24 + 16, :]
                for j in range(1, 9):
                    mixed = mixed + crossing[j] * filt[w, i * 24 + 8 + j : i * 24 + 16 + j, :]
                squares = squares + mixed * mixed
            raw[t, 24:32, :] = squares
            return carry

        lax.fori_loop(0, CW, body, 0, unroll=2)
        left = jnp.concatenate([rim[:, pl.ds(pl.multiple_of((first + t) * NFFT, LANES), NFFT + LANES)] for t in range(CW)], axis=0)
        parts = dot(left, fold_w[...])
        rim_raw = parts[:, 0:LANES] + parts[:, LANES:]
        pieces = []
        for t in range(CW):
            raw[t, 0:16, :] = own_raw[k, t * 16 : t * 16 + 16, :]
            raw[t, 16:24, :] = rim_raw[t * 8 : t * 8 + 8]
            lower = weights[0] * raw[t, 0:8, :]
            upper = crossing[0] * raw[t, 8:16, :]
            for j in range(1, 9):
                lower = lower + weights[j] * raw[t, j : j + 8, :]
                upper = upper + crossing[j] * raw[t, 8 + j : 16 + j, :]
            for value, squares in ((lower, power_low[first + t]), (upper, raw[t, 24:32, :])):
                mean = jnp.sum(squares, axis=1, keepdims=True) * (1.0 / NFFT)
                pieces.append(value / jnp.sqrt(mean + EPSILON))
        spectra = jnp.concatenate(pieces, axis=0).astype(BF16)
        spread = dot(spectra[:, 0 : 2 * BINS], tab[2 * LANES : 2 * LANES + 2 * BINS])
        rows, lanes = iota((LANES, LANES), 0), iota((LANES, LANES), 1)
        mine = lax.rem(lax.rem(rows, 16) + 4, 16) == lanes // GROUP
        columns = [
            jnp.where(mine, spread[:, g * LANES : (g + 1) * LANES], 0.0).astype(BF16) for g in range(8)
        ]
        stacked = jnp.concatenate(
            [jnp.concatenate(columns[0:4], axis=1), jnp.concatenate(columns[4:8], axis=1)], axis=0
        )
        collect = jnp.where(
            iota((16, 256), 0) == iota((16, 256), 1) // 16, 1.0, 0.0
        ).astype(BF16)
        packed = dot(collect, stacked).astype(BF16)
        for g in range(reps):
            packs[k, g] = packed[:, g * LANES : (g + 1) * LANES]
        gathered[1, k, r] = packs[k, r]

    def first_copy(k, d):
        return pltpu.make_async_remote_copy(
            packs.at[k, rep_at(d)], gathered.at[1, k, r], one_send.at[k, d - 1], one_recv.at[k, d - 1],
            device_id={"chan": b, "rep": rep_at(d)}, device_id_type=MESH,
        )

    def second_copy(k, s):
        slot = 0 if s == 0 else s + 1
        return pltpu.make_async_remote_copy(
            gathered.at[1, k], gathered.at[slot, k], two_send.at[k, s], two_recv.at[k, s],
            device_id={"chan": block_at(1 if s == 0 else -s), "rep": r}, device_id_type=MESH,
        )

    def lower_body(step, carry):
        k = lax.rem(step + 1, chunks)

        @pl.when(step == chunks - 1)
        def _():
            hist_own.wait_recv()

            @pl.when(r == 0)
            def _():
                own[:, 0:LANES] = jnp.zeros((16, LANES), BF16)

        lower_chunk(k)
        return carry

    lax.fori_loop(0, chunks, lower_body, 0)

    def forward(k):
        for d in range(1, reps):
            first_copy(k, d).wait_recv()
        for s in range(5):
            second_copy(k, s).start()

    hist_rim.wait_recv()

    @pl.when(r == 0)
    def _():
        rim[:, 0:LANES] = jnp.zeros((8, LANES), BF16)

    def upper_body(k, carry):
        rim_copy(k).wait_recv()
        upper_chunk(k)
        for d in range(1, reps):
            first_copy(k, d).start()

        @pl.when(k > 0)
        def _():
            forward(k - 1)

        return carry

    lax.fori_loop(0, chunks, upper_body, 0)
    forward(chunks - 1)
    for k in range(chunks):
        for s in range(5):
            second_copy(k, s).wait_recv()

    depth = chunks * reps * 16
    own_lanes = iota((depth, LANES), 1) < 32

    def merged(s):
        return jnp.where(
            own_lanes,
            gathered[s].reshape(depth, LANES).astype(F32),
            gathered[s + 1].reshape(depth, LANES).astype(F32),
        )

    mine = merged(0)
    cubes = mine.reshape(chunks * reps, 2, 8, LANES)
    swapped = jnp.concatenate([cubes[:, 1:2], -cubes[:, 0:1]], axis=1).reshape(depth, LANES)
    left = jnp.concatenate([mine.T, swapped.T], axis=0).astype(BF16)
    same_bin = lax.rem(iota((LANES, LANES), 0), GROUP) == lax.rem(iota((LANES, LANES), 1), GROUP)
    pick_row, pick_lane = iota((LANES, LANES), 0), iota((LANES, LANES), 1)
    pick_real = jnp.where(pick_lane == pick_row // GROUP, 1.0, 0.0).astype(BF16)
    pick_imag = jnp.where(pick_lane == 16 + pick_row // GROUP, 1.0, 0.0).astype(BF16)
    picks = jnp.concatenate([pick_real, pick_imag] * 3, axis=0)
    scale = 1.0 / (windows * reps)
    for s in range(5):
        block = (mine if s == 0 else merged(s)).astype(BF16)
        product = dot(left, block)
        real = jnp.where(same_bin, product[0:LANES], 0.0) * scale
        imag = jnp.where(same_bin, product[LANES:], 0.0) * scale
        terms = []
        for _ in range(3):
            real_part, imag_part = real.astype(BF16), imag.astype(BF16)
            terms += [real_part, imag_part]
            real, imag = real - real_part.astype(F32), imag - imag_part.astype(F32)
        tile = dot(jnp.concatenate(terms, axis=1), picks)
        for c in range(16):
            out[c, s] = tile[c * GROUP : (c + 1) * GROUP, 0:32]

    for k in range(chunks):
        rim_copy(k).wait_send()
        for d in range(1, reps):
            first_copy(k, d).wait_send()
        for s in range(5):
            second_copy(k, s).wait_send()
    hist_own.wait_send()
    hist_rim.wait_send()


def solution(mesh):
    chans, reps = mesh.shape["chan"], mesh.shape["rep"]

    def per_device(strain, fir_taps, spatial):
        rows, samples = strain.shape
        windows = samples // NFFT
        chunks = windows // CW
        anywhere = pl.BlockSpec(memory_space=pl.ANY)
        return pl.pallas_call(
            functools.partial(kernel, chans, reps),
            out_shape=jax.ShapeDtypeStruct((rows, 5, BINS // reps, 32), F32),
            in_specs=[anywhere] * 4,
            out_specs=pl.BlockSpec(memory_space=pltpu.VMEM),
            scratch_shapes=[
                pltpu.VMEM((1, fir_taps.shape[0]), F32),
                pltpu.SMEM(spatial.shape, F32),
                pltpu.VMEM((rows, samples + LANES), BF16),
                pltpu.VMEM((8, samples + LANES), BF16),
                pltpu.VMEM((2 * LANES, 2 * LANES), BF16),
                pltpu.VMEM((NFFT + LANES, 2 * LANES), BF16),
                pltpu.VMEM((2 * LANES + 2 * BINS, 1024), BF16),
                pltpu.VMEM((windows, 192, LANES), F32),
                pltpu.VMEM((CW, 32, LANES), F32),
                pltpu.VMEM((windows, 8, LANES), F32),
                pltpu.VMEM((chunks, CW * 16, LANES), F32),
                pltpu.VMEM((chunks, reps, 16, LANES), BF16),
                pltpu.VMEM((6, chunks, reps, 16, LANES), BF16),
                pltpu.VMEM((8, LANES), F32),
                pltpu.SemaphoreType.DMA((4,)),
                pltpu.SemaphoreType.DMA((chunks,)),
                pltpu.SemaphoreType.DMA((chunks,)),
                pltpu.SemaphoreType.DMA((2,)),
                pltpu.SemaphoreType.DMA((2,)),
                pltpu.SemaphoreType.DMA((chunks, 3)),
                pltpu.SemaphoreType.DMA((chunks, 3)),
                pltpu.SemaphoreType.DMA((chunks, 5)),
                pltpu.SemaphoreType.DMA((chunks, 5)),
            ],
            compiler_params=pltpu.CompilerParams(
                collective_id=0, has_side_effects=True, vmem_limit_bytes=67043328
            ),
        )(strain, fir_taps.reshape(1, -1), spatial, jnp.asarray(tables()))

    return jax.shard_map(
        per_device,
        mesh=mesh,
        in_specs=(P("chan", "rep"), P(), P()),
        out_specs=P("chan", None, "rep", None),
        check_vma=False,
    )
```

```python
import functools
import math

import jax
import jax.numpy as jnp
import ml_dtypes
import numpy as np
from jax import lax
from jax.experimental import pallas as pl
from jax.experimental.pallas import tpu as pltpu
from jax.sharding import PartitionSpec as P

NFFT = 1024
BINS = 32
FIRST_BIN = 16
EPSILON = 1e-05
LANES = 128
CW = 8
GROUP = 8
BLOCKS_PER_WINDOW = NFFT // LANES
MESH = pl.DeviceIdType.MESH
F32 = jnp.float32
BF16 = jnp.bfloat16


def split_table(values):
    high = values.astype(ml_dtypes.bfloat16)
    low = (values - high.astype(np.float64)).astype(ml_dtypes.bfloat16)
    return high, low


def tables():
    sample = np.arange(LANES)[:, None, None]
    block = np.arange(BLOCKS_PER_WINDOW)[None, :, None]
    bins = (FIRST_BIN + np.arange(BINS))[None, None, :]
    angle = ((block * LANES + sample) * bins % NFFT) * (2.0 * math.pi / NFFT)
    parts = np.concatenate([np.cos(angle), -np.sin(angle)], axis=2) / math.sqrt(NFFT)
    parts = np.concatenate([parts, np.zeros_like(parts)], axis=2)
    high, low = split_table(parts.reshape(LANES, BLOCKS_PER_WINDOW * LANES))
    row = np.arange(2 * BINS)[:, None]
    lane = np.arange(1024)[None, :]
    source = (lane // 512) * BINS + (lane % 512) // LANES * GROUP + lane % GROUP
    choose = (row == source).astype(ml_dtypes.bfloat16)
    return np.concatenate([high, low, choose], axis=0)


def iota(shape, dim):
    return lax.broadcasted_iota(jnp.int32, shape, dim)


def dot(a, b):
    return jnp.dot(a, b, preferred_element_type=F32)


def kernel(
    chans, reps, strain, taps_in, spatial_in, table, out,
    taps, spatial, own, rim, fir_w, fold_w, tab, filt, raw, power_low, own_raw, packs, gathered, near, near_in,
    local_sem, rim_send, rim_recv, hist_send, hist_recv, one_send, one_recv, two_send, two_recv,
):
    b = lax.axis_index("chan")
    r = lax.axis_index("rep")
    samples = strain.shape[1]
    windows = samples // NFFT
    chunks = windows // CW
    span = CW * NFFT

    def block_at(step):
        return lax.rem(b + (step + chans), chans)

    def rep_at(step):
        return lax.rem(r + (step + reps), reps)

    barrier = pltpu.get_barrier_semaphore()
    peers = [(s, 0) for s in (-4, -3, -2, -1, 1, 2, 3, 4)] + [(0, d) for d in range(1, reps)] + [(-1, 1), (1, -1)]
    for s, d in peers:
        pl.semaphore_signal(
            barrier, inc=1, device_id={"chan": block_at(s), "rep": rep_at(d)}, device_id_type=MESH
        )
    fetch_own = pltpu.make_async_copy(strain, own.at[:, pl.ds(LANES, samples)], local_sem.at[0])
    fetch_own.start()
    fetch_spatial = pltpu.make_async_copy(spatial_in, spatial, local_sem.at[2])
    fetch_spatial.start()
    fetch_taps = pltpu.make_async_copy(taps_in, taps, local_sem.at[3])
    fetch_taps.start()
    fetch_tab = pltpu.make_async_copy(table, tab, local_sem.at[1])
    fetch_tab.start()

    pl.semaphore_wait(barrier, len(peers))

    def rim_copy(k):
        return pltpu.make_async_remote_copy(
            strain.at[pl.ds(0, 8), pl.ds(k * span, span)],
            rim.at[:, pl.ds(pl.multiple_of(LANES + k * span, LANES), span)],
            rim_send.at[k], rim_recv.at[k],
            device_id={"chan": block_at(-1), "rep": r}, device_id_type=MESH,
        )

    hist_own = pltpu.make_async_remote_copy(
        strain.at[:, pl.ds(samples - LANES, LANES)], own.at[:, pl.ds(0, LANES)],
        hist_send.at[0], hist_recv.at[0],
        device_id={"chan": b, "rep": rep_at(1)}, device_id_type=MESH,
    )
    hist_rim = pltpu.make_async_remote_copy(
        strain.at[pl.ds(0, 8), pl.ds(samples - LANES, LANES)], rim.at[:, pl.ds(0, LANES)],
        hist_send.at[1], hist_recv.at[1],
        device_id={"chan": block_at(-1), "rep": rep_at(1)}, device_id_type=MESH,
    )
    hist_own.start()
    hist_rim.start()
    for k in range(chunks):
        rim_copy(k).start()

    row, lane = iota((LANES, LANES), 0), iota((LANES, LANES), 1)
    fetch_taps.wait()
    tap_row = jnp.concatenate([taps[...], jnp.zeros((1, LANES - taps.shape[1]), F32)], axis=1)
    circulant = pltpu.roll(jnp.broadcast_to(tap_row, (LANES, LANES)), 0, 1, stride=1, stride_axis=0)
    now = jnp.where(lane >= row, circulant, 0.0)
    before = jnp.where(lane < row, circulant, 0.0)
    both = jnp.concatenate([before, now], axis=0)
    both_high = both.astype(BF16)
    both_low = (both - both_high.astype(F32)).astype(BF16)
    fir_w[:, 0:LANES] = both_high
    fir_w[:, LANES:] = both_low
    fetch_tab.wait()
    folded = dot(
        jnp.concatenate([both_high, both_low, both_high], axis=1),
        jnp.concatenate([tab[0:LANES], tab[0:LANES], tab[LANES : 2 * LANES]], axis=0),
    )
    for q in range(BLOCKS_PER_WINDOW + 1):
        part = jnp.zeros((LANES, LANES), F32)
        if q > 0:
            part = part + folded[LANES:, (q - 1) * LANES : q * LANES]
        if q < BLOCKS_PER_WINDOW:
            part = part + folded[0:LANES, q * LANES : (q + 1) * LANES]
        part_high = part.astype(BF16)
        fold_w[q * LANES : (q + 1) * LANES, 0:LANES] = part_high
        fold_w[q * LANES : (q + 1) * LANES, LANES:] = (part - part_high.astype(F32)).astype(BF16)

    half_row = iota((8, LANES), 0)
    fetch_spatial.wait()
    weights = [spatial[j] for j in range(9)]
    crossing = []
    for j in range(9):
        same = (half_row < 4) == (half_row + (8 + j) < 16)
        keep = jnp.logical_or(same, b != chans - 1)
        crossing.append(jnp.where(keep, weights[j], 0.0))

    fetch_own.wait()

    def lower_window(w):
        base = pl.multiple_of(w * NFFT, LANES)
        left = jnp.concatenate([own[:, pl.ds(base + i * LANES, 2 * LANES)] for i in range(BLOCKS_PER_WINDOW)], axis=0)
        both_parts = dot(left, fir_w[...])
        band = both_parts[:, 0:LANES] + both_parts[:, LANES:]
        for i in range(BLOCKS_PER_WINDOW):
            filt[w, i * 24 : i * 24 + 16, :] = band[i * 16 : i * 16 + 16]
        squares = jnp.zeros((8, LANES), F32)
        for i in range(BLOCKS_PER_WINDOW):
            mixed = weights[0] * filt[w, i * 24 : i * 24 + 8, :]
            for j in range(1, 9):
                mixed = mixed + weights[j] * filt[w, i * 24 + j : i * 24 + j + 8, :]
            squares = squares + mixed * mixed
        power_low[w] = squares

    def lower_chunk(k):
        first = k * CW

        def body(t, carry):
            lower_window(first + t)
            return carry

        lax.fori_loop(0, CW, body, 0, unroll=2)
        left = jnp.concatenate(
            [own[:, pl.ds(pl.multiple_of((first + t) * NFFT, LANES), NFFT + LANES)] for t in range(CW)], axis=0
        )
        parts = dot(left, fold_w[...])
        own_raw[k] = parts[:, 0:LANES] + parts[:, LANES:]

    def upper_chunk(k):
        first = k * CW

        def body(t, carry):
            w = first + t
            base = pl.multiple_of(w * NFFT, LANES)
            left = jnp.concatenate(
                [rim[:, pl.ds(base + i * LANES, 2 * LANES)] for i in range(BLOCKS_PER_WINDOW)], axis=0
            )
            both_parts = dot(left, fir_w[...])
            band = both_parts[:, 0:LANES] + both_parts[:, LANES:]
            for i in range(BLOCKS_PER_WINDOW):
                filt[w, i * 24 + 16 : i * 24 + 24, :] = band[i * 8 : i * 8 + 8]
            squares = jnp.zeros((8, LANES), F32)
            for i in range(BLOCKS_PER_WINDOW):
                mixed = crossing[0] * filt[w, i * 24 + 8 : i * 24 + 16, :]
                for j in range(1, 9):
                    mixed = mixed + crossing[j] * filt[w, i * 24 + 8 + j : i * 24 + 16 + j, :]
                squares = squares + mixed * mixed
            raw[t, 24:32, :] = squares
            return carry

        lax.fori_loop(0, CW, body, 0, unroll=2)
        left = jnp.concatenate([rim[:, pl.ds(pl.multiple_of((first + t) * NFFT, LANES), NFFT + LANES)] for t in range(CW)], axis=0)
        parts = dot(left, fold_w[...])
        rim_raw = parts[:, 0:LANES] + parts[:, LANES:]
        pieces = []
        for t in range(CW):
            raw[t, 0:16, :] = own_raw[k, t * 16 : t * 16 + 16, :]
            raw[t, 16:24, :] = rim_raw[t * 8 : t * 8 + 8]
            lower = weights[0] * raw[t, 0:8, :]
            upper = crossing[0] * raw[t, 8:16, :]
            for j in range(1, 9):
                lower = lower + weights[j] * raw[t, j : j + 8, :]
                upper = upper + crossing[j] * raw[t, 8 + j : 16 + j, :]
            for value, squares in ((lower, power_low[first + t]), (upper, raw[t, 24:32, :])):
                mean = jnp.sum(squares, axis=1, keepdims=True) * (1.0 / NFFT)
                pieces.append(value / jnp.sqrt(mean + EPSILON))
        spectra = jnp.concatenate(pieces, axis=0).astype(BF16)
        spread = dot(spectra[:, 0 : 2 * BINS], tab[2 * LANES : 2 * LANES + 2 * BINS])
        rows, lanes = iota((LANES, LANES), 0), iota((LANES, LANES), 1)
        mine = lax.rem(lax.rem(rows, 16) + 4, 16) == lanes // GROUP
        columns = [
            jnp.where(mine, spread[:, g * LANES : (g + 1) * LANES], 0.0).astype(BF16) for g in range(8)
        ]
        stacked = jnp.concatenate(
            [jnp.concatenate(columns[0:4], axis=1), jnp.concatenate(columns[4:8], axis=1)], axis=0
        )
        collect = jnp.where(
            iota((16, 256), 0) == iota((16, 256), 1) // 16, 1.0, 0.0
        ).astype(BF16)
        packed = dot(collect, stacked).astype(BF16)
        for g in range(reps):
            packs[k, g] = packed[:, g * LANES : (g + 1) * LANES]
        gathered[0, k, r] = packs[k, r]

    def first_copy(k, d):
        return pltpu.make_async_remote_copy(
            packs.at[k, rep_at(d)], gathered.at[0, k, r], one_send.at[k, d - 1], one_recv.at[k, d - 1],
            device_id={"chan": b, "rep": rep_at(d)}, device_id_type=MESH,
        )

    def second_copy(k, s):
        source, target, step = (near, near_in, 1) if s == 0 else (gathered.at[0], gathered.at[s], -s)
        return pltpu.make_async_remote_copy(
            source.at[k], target.at[k], two_send.at[k, s], two_recv.at[k, s],
            device_id={"chan": block_at(step), "rep": r}, device_id_type=MESH,
        )

    def lower_body(step, carry):
        k = lax.rem(step + 1, chunks)

        @pl.when(step == chunks - 1)
        def _():
            hist_own.wait_recv()

            @pl.when(r == 0)
            def _():
                own[:, 0:LANES] = jnp.zeros((16, LANES), BF16)

        lower_chunk(k)
        return carry

    lax.fori_loop(0, chunks, lower_body, 0)

    def forward(k):
        for d in range(1, reps):
            first_copy(k, d).wait_recv()
        for s in range(1, 5):
            second_copy(k, s).start()
        quarter = iota((16, LANES), 1) // 32
        side = jnp.zeros((16, LANES), F32)
        for g in range(reps):
            part = gathered[0, k, g].astype(F32)
            side = jnp.where(quarter == g, part if g == 0 else pltpu.roll(part, 32 * g, 1), side)
        near[k] = side.astype(BF16)
        second_copy(k, 0).start()

    hist_rim.wait_recv()

    @pl.when(r == 0)
    def _():
        rim[:, 0:LANES] = jnp.zeros((8, LANES), BF16)

    def upper_body(k, carry):
        rim_copy(k).wait_recv()
        upper_chunk(k)
        for d in range(1, reps):
            first_copy(k, d).start()
        return carry

    lax.fori_loop(0, chunks, upper_body, 0)
    for k in range(chunks):
        forward(k)
    for k in range(chunks):
        for s in range(5):
            second_copy(k, s).wait_recv()

    depth = chunks * reps * 16
    own_lanes = iota((depth, LANES), 1) < 32

    def block_of(s):
        return gathered[s].reshape(depth, LANES).astype(F32)

    def merged(s):
        return jnp.where(own_lanes, block_of(s - 1), block_of(s))

    own_first = []
    for k in range(chunks):
        side = near_in[k].astype(F32)
        for g in range(reps):
            own_first.append(side if g == 0 else pltpu.roll(side, LANES - 32 * g, 1))
    mine = jnp.where(own_lanes, jnp.concatenate(own_first, axis=0), block_of(0))
    cubes = mine.reshape(chunks * reps, 2, 8, LANES)
    swapped = jnp.concatenate([cubes[:, 1:2], -cubes[:, 0:1]], axis=1).reshape(depth, LANES)
    left = jnp.concatenate([mine.T, swapped.T], axis=0).astype(BF16)
    same_bin = lax.rem(iota((LANES, LANES), 0), GROUP) == lax.rem(iota((LANES, LANES), 1), GROUP)
    pick_row, pick_lane = iota((LANES, LANES), 0), iota((LANES, LANES), 1)
    pick_real = jnp.where(pick_lane == pick_row // GROUP, 1.0, 0.0).astype(BF16)
    pick_imag = jnp.where(pick_lane == 16 + pick_row // GROUP, 1.0, 0.0).astype(BF16)
    picks = jnp.concatenate([pick_real, pick_imag] * 3, axis=0)
    scale = 1.0 / (windows * reps)
    for s in range(5):
        block = (mine if s == 0 else merged(s)).astype(BF16)
        product = dot(left, block)
        real = jnp.where(same_bin, product[0:LANES], 0.0) * scale
        imag = jnp.where(same_bin, product[LANES:], 0.0) * scale
        terms = []
        for _ in range(3):
            real_part, imag_part = real.astype(BF16), imag.astype(BF16)
            terms += [real_part, imag_part]
            real, imag = real - real_part.astype(F32), imag - imag_part.astype(F32)
        tile = dot(jnp.concatenate(terms, axis=1), picks)
        for c in range(16):
            out[c, s] = tile[c * GROUP : (c + 1) * GROUP, 0:32]

    for k in range(chunks):
        rim_copy(k).wait_send()
        for d in range(1, reps):
            first_copy(k, d).wait_send()
        for s in range(5):
            second_copy(k, s).wait_send()
    hist_own.wait_send()
    hist_rim.wait_send()


def solution(mesh):
    chans, reps = mesh.shape["chan"], mesh.shape["rep"]

    def per_device(strain, fir_taps, spatial):
        rows, samples = strain.shape
        windows = samples // NFFT
        chunks = windows // CW
        anywhere = pl.BlockSpec(memory_space=pl.ANY)
        return pl.pallas_call(
            functools.partial(kernel, chans, reps),
            out_shape=jax.ShapeDtypeStruct((rows, 5, BINS // reps, 32), F32),
            in_specs=[anywhere] * 4,
            out_specs=pl.BlockSpec(memory_space=pltpu.VMEM),
            scratch_shapes=[
                pltpu.VMEM((1, fir_taps.shape[0]), F32),
                pltpu.SMEM(spatial.shape, F32),
                pltpu.VMEM((rows, samples + LANES), BF16),
                pltpu.VMEM((8, samples + LANES), BF16),
                pltpu.VMEM((2 * LANES, 2 * LANES), BF16),
                pltpu.VMEM((NFFT + LANES, 2 * LANES), BF16),
                pltpu.VMEM((2 * LANES + 2 * BINS, 1024), BF16),
                pltpu.VMEM((windows, 192, LANES), F32),
                pltpu.VMEM((CW, 32, LANES), F32),
                pltpu.VMEM((windows, 8, LANES), F32),
                pltpu.VMEM((chunks, CW * 16, LANES), F32),
                pltpu.VMEM((chunks, reps, 16, LANES), BF16),
                pltpu.VMEM((5, chunks, reps, 16, LANES), BF16),
                pltpu.VMEM((chunks, 16, LANES), BF16),
                pltpu.VMEM((chunks, 16, LANES), BF16),
                pltpu.SemaphoreType.DMA((4,)),
                pltpu.SemaphoreType.DMA((chunks,)),
                pltpu.SemaphoreType.DMA((chunks,)),
                pltpu.SemaphoreType.DMA((2,)),
                pltpu.SemaphoreType.DMA((2,)),
                pltpu.SemaphoreType.DMA((chunks, 3)),
                pltpu.SemaphoreType.DMA((chunks, 3)),
                pltpu.SemaphoreType.DMA((chunks, 5)),
                pltpu.SemaphoreType.DMA((chunks, 5)),
            ],
            compiler_params=pltpu.CompilerParams(
                collective_id=0, has_side_effects=True, vmem_limit_bytes=67043328
            ),
        )(strain, fir_taps.reshape(1, -1), spatial, jnp.asarray(tables()))

    return jax.shard_map(
        per_device,
        mesh=mesh,
        in_specs=(P("chan", "rep"), P(), P()),
        out_specs=P("chan", None, "rep", None),
        check_vma=False,
    )
```

```python
import functools
import math

import jax
import jax.numpy as jnp
import ml_dtypes
import numpy as np
from jax import lax
from jax.experimental import pallas as pl
from jax.experimental.pallas import tpu as pltpu
from jax.sharding import PartitionSpec as P

NFFT = 1024
BINS = 32
FIRST_BIN = 16
EPSILON = 1e-05
LANES = 128
CW = 8
GROUP = 8
BLOCKS_PER_WINDOW = NFFT // LANES
MESH = pl.DeviceIdType.MESH
F32 = jnp.float32
BF16 = jnp.bfloat16


def split_table(values):
    high = values.astype(ml_dtypes.bfloat16)
    low = (values - high.astype(np.float64)).astype(ml_dtypes.bfloat16)
    return high, low


def tables():
    sample = np.arange(LANES)[:, None, None]
    block = np.arange(BLOCKS_PER_WINDOW)[None, :, None]
    bins = (FIRST_BIN + np.arange(BINS))[None, None, :]
    angle = ((block * LANES + sample) * bins % NFFT) * (2.0 * math.pi / NFFT)
    parts = np.concatenate([np.cos(angle), -np.sin(angle)], axis=2) / math.sqrt(NFFT)
    parts = np.concatenate([parts, np.zeros_like(parts)], axis=2)
    high, low = split_table(parts.reshape(LANES, BLOCKS_PER_WINDOW * LANES))
    row = np.arange(2 * BINS)[:, None]
    lane = np.arange(1024)[None, :]
    source = (lane // 512) * BINS + (lane % 512) // LANES * GROUP + lane % GROUP
    choose = (row == source).astype(ml_dtypes.bfloat16)
    return np.concatenate([high, low, choose], axis=0)


def iota(shape, dim):
    return lax.broadcasted_iota(jnp.int32, shape, dim)


def dot(a, b):
    return jnp.dot(a, b, preferred_element_type=F32)


def kernel(
    chans, reps, strain, taps_in, spatial_in, table, out,
    taps, spatial, own, rim, fir_w, fold_w, tab, filt, raw, power_low, own_raw, packs, gathered, tiles,
    local_sem, rim_send, rim_recv, hist_send, hist_recv, one_send, one_recv, two_send, two_recv,
):
    b = lax.axis_index("chan")
    r = lax.axis_index("rep")
    samples = strain.shape[1]
    windows = samples // NFFT
    chunks = windows // CW
    span = CW * NFFT

    def block_at(step):
        return lax.rem(b + (step + chans), chans)

    def rep_at(step):
        return lax.rem(r + (step + reps), reps)

    barrier = pltpu.get_barrier_semaphore()
    peers = [(s, 0) for s in (-4, -3, -2, -1, 1, 2, 3, 4)] + [(0, d) for d in range(1, reps)] + [(-1, 1), (1, -1)]
    for s, d in peers:
        pl.semaphore_signal(
            barrier, inc=1, device_id={"chan": block_at(s), "rep": rep_at(d)}, device_id_type=MESH
        )
    fetch_own = pltpu.make_async_copy(strain, own.at[:, pl.ds(LANES, samples)], local_sem.at[0])
    fetch_own.start()
    fetch_spatial = pltpu.make_async_copy(spatial_in, spatial, local_sem.at[2])
    fetch_spatial.start()
    fetch_taps = pltpu.make_async_copy(taps_in, taps, local_sem.at[3])
    fetch_taps.start()
    fetch_tab = pltpu.make_async_copy(table, tab, local_sem.at[1])
    fetch_tab.start()

    pl.semaphore_wait(barrier, len(peers))

    def rim_copy(k):
        return pltpu.make_async_remote_copy(
            strain.at[pl.ds(0, 8), pl.ds(k * span, span)],
            rim.at[:, pl.ds(pl.multiple_of(LANES + k * span, LANES), span)],
            rim_send.at[k], rim_recv.at[k],
            device_id={"chan": block_at(-1), "rep": r}, device_id_type=MESH,
        )

    hist_own = pltpu.make_async_remote_copy(
        strain.at[:, pl.ds(samples - LANES, LANES)], own.at[:, pl.ds(0, LANES)],
        hist_send.at[0], hist_recv.at[0],
        device_id={"chan": b, "rep": rep_at(1)}, device_id_type=MESH,
    )
    hist_rim = pltpu.make_async_remote_copy(
        strain.at[pl.ds(0, 8), pl.ds(samples - LANES, LANES)], rim.at[:, pl.ds(0, LANES)],
        hist_send.at[1], hist_recv.at[1],
        device_id={"chan": block_at(-1), "rep": rep_at(1)}, device_id_type=MESH,
    )
    hist_own.start()
    hist_rim.start()
    for k in range(chunks):
        rim_copy(k).start()

    row, lane = iota((LANES, LANES), 0), iota((LANES, LANES), 1)
    fetch_taps.wait()
    tap_row = jnp.concatenate([taps[...], jnp.zeros((1, LANES - taps.shape[1]), F32)], axis=1)
    circulant = pltpu.roll(jnp.broadcast_to(tap_row, (LANES, LANES)), 0, 1, stride=1, stride_axis=0)
    now = jnp.where(lane >= row, circulant, 0.0)
    before = jnp.where(lane < row, circulant, 0.0)
    both = jnp.concatenate([before, now], axis=0)
    both_high = both.astype(BF16)
    both_low = (both - both_high.astype(F32)).astype(BF16)
    fir_w[:, 0:LANES] = both_high
    fir_w[:, LANES:] = both_low
    fetch_tab.wait()
    folded = dot(
        jnp.concatenate([both_high, both_low, both_high], axis=1),
        jnp.concatenate([tab[0:LANES], tab[0:LANES], tab[LANES : 2 * LANES]], axis=0),
    )
    for q in range(BLOCKS_PER_WINDOW + 1):
        part = jnp.zeros((LANES, LANES), F32)
        if q > 0:
            part = part + folded[LANES:, (q - 1) * LANES : q * LANES]
        if q < BLOCKS_PER_WINDOW:
            part = part + folded[0:LANES, q * LANES : (q + 1) * LANES]
        part_high = part.astype(BF16)
        fold_w[q * LANES : (q + 1) * LANES, 0:LANES] = part_high
        fold_w[q * LANES : (q + 1) * LANES, LANES:] = (part - part_high.astype(F32)).astype(BF16)

    half_row = iota((8, LANES), 0)
    fetch_spatial.wait()
    weights = [spatial[j] for j in range(9)]
    crossing = []
    for j in range(9):
        same = (half_row < 4) == (half_row + (8 + j) < 16)
        keep = jnp.logical_or(same, b != chans - 1)
        crossing.append(jnp.where(keep, weights[j], 0.0))

    fetch_own.wait()

    def lower_window(w):
        base = pl.multiple_of(w * NFFT, LANES)
        left = jnp.concatenate([own[:, pl.ds(base + i * LANES, 2 * LANES)] for i in range(BLOCKS_PER_WINDOW)], axis=0)
        both_parts = dot(left, fir_w[...])
        band = both_parts[:, 0:LANES] + both_parts[:, LANES:]
        for i in range(BLOCKS_PER_WINDOW):
            filt[w, i * 24 : i * 24 + 16, :] = band[i * 16 : i * 16 + 16]
        squares = jnp.zeros((8, LANES), F32)
        for i in range(BLOCKS_PER_WINDOW):
            mixed = weights[0] * filt[w, i * 24 : i * 24 + 8, :]
            for j in range(1, 9):
                mixed = mixed + weights[j] * filt[w, i * 24 + j : i * 24 + j + 8, :]
            squares = squares + mixed * mixed
        power_low[w] = squares

    def lower_chunk(k):
        first = k * CW

        def body(t, carry):
            lower_window(first + t)
            return carry

        lax.fori_loop(0, CW, body, 0, unroll=4)
        left = jnp.concatenate(
            [own[:, pl.ds(pl.multiple_of((first + t) * NFFT, LANES), NFFT + LANES)] for t in range(CW)], axis=0
        )
        parts = dot(left, fold_w[...])
        own_raw[k] = parts[:, 0:LANES] + parts[:, LANES:]

    def upper_chunk(k):
        first = k * CW

        def body(t, carry):
            w = first + t
            base = pl.multiple_of(w * NFFT, LANES)
            left = jnp.concatenate(
                [rim[:, pl.ds(base + i * LANES, 2 * LANES)] for i in range(BLOCKS_PER_WINDOW)], axis=0
            )
            both_parts = dot(left, fir_w[...])
            band = both_parts[:, 0:LANES] + both_parts[:, LANES:]
            for i in range(BLOCKS_PER_WINDOW):
                filt[w, i * 24 + 16 : i * 24 + 24, :] = band[i * 8 : i * 8 + 8]
            squares = jnp.zeros((8, LANES), F32)
            for i in range(BLOCKS_PER_WINDOW):
                mixed = crossing[0] * filt[w, i * 24 + 8 : i * 24 + 16, :]
                for j in range(1, 9):
                    mixed = mixed + crossing[j] * filt[w, i * 24 + 8 + j : i * 24 + 16 + j, :]
                squares = squares + mixed * mixed
            raw[t, 24:32, :] = squares
            return carry

        lax.fori_loop(0, CW, body, 0, unroll=4)
        left = jnp.concatenate([rim[:, pl.ds(pl.multiple_of((first + t) * NFFT, LANES), NFFT + LANES)] for t in range(CW)], axis=0)
        parts = dot(left, fold_w[...])
        rim_raw = parts[:, 0:LANES] + parts[:, LANES:]
        pieces = []
        for t in range(CW):
            raw[t, 0:16, :] = own_raw[k, t * 16 : t * 16 + 16, :]
            raw[t, 16:24, :] = rim_raw[t * 8 : t * 8 + 8]
            lower = weights[0] * raw[t, 0:8, :]
            upper = crossing[0] * raw[t, 8:16, :]
            for j in range(1, 9):
                lower = lower + weights[j] * raw[t, j : j + 8, :]
                upper = upper + crossing[j] * raw[t, 8 + j : 16 + j, :]
            for value, squares in ((lower, power_low[first + t]), (upper, raw[t, 24:32, :])):
                mean = jnp.sum(squares, axis=1, keepdims=True) * (1.0 / NFFT)
                pieces.append(value / jnp.sqrt(mean + EPSILON))
        spectra = jnp.concatenate(pieces, axis=0).astype(BF16)
        spread = dot(spectra[:, 0 : 2 * BINS], tab[2 * LANES : 2 * LANES + 2 * BINS])
        rows, lanes = iota((LANES, LANES), 0), iota((LANES, LANES), 1)
        mine = lax.rem(lax.rem(rows, 16) + 4, 16) == lanes // GROUP
        columns = [
            jnp.where(mine, spread[:, g * LANES : (g + 1) * LANES], 0.0).astype(BF16) for g in range(8)
        ]
        stacked = jnp.concatenate(
            [jnp.concatenate(columns[0:4], axis=1), jnp.concatenate(columns[4:8], axis=1)], axis=0
        )
        collect = jnp.where(
            iota((16, 256), 0) == iota((16, 256), 1) // 16, 1.0, 0.0
        ).astype(BF16)
        packed = dot(collect, stacked).astype(BF16)
        for g in range(reps):
            packs[k, g] = packed[:, g * LANES : (g + 1) * LANES]
        gathered[1, k, r] = packs[k, r]

    def first_copy(k, d):
        return pltpu.make_async_remote_copy(
            packs.at[k, rep_at(d)], gathered.at[1, k, r], one_send.at[k, d - 1], one_recv.at[k, d - 1],
            device_id={"chan": b, "rep": rep_at(d)}, device_id_type=MESH,
        )

    def second_copy(k, s):
        slot = 0 if s == 0 else s + 1
        return pltpu.make_async_remote_copy(
            gathered.at[1, k], gathered.at[slot, k], two_send.at[k, s], two_recv.at[k, s],
            device_id={"chan": block_at(1 if s == 0 else -s), "rep": r}, device_id_type=MESH,
        )

    def lower_body(step, carry):
        k = lax.rem(step + 1, chunks)

        @pl.when(step == chunks - 1)
        def _():
            hist_own.wait_recv()

            @pl.when(r == 0)
            def _():
                own[:, 0:LANES] = jnp.zeros((16, LANES), BF16)

        lower_chunk(k)
        return carry

    lax.fori_loop(0, chunks, lower_body, 0)

    def forward(k):
        for d in range(1, reps):
            first_copy(k, d).wait_recv()
        for s in range(5):
            second_copy(k, s).start()

    hist_rim.wait_recv()

    @pl.when(r == 0)
    def _():
        rim[:, 0:LANES] = jnp.zeros((8, LANES), BF16)

    def upper_body(k, carry):
        rim_copy(k).wait_recv()
        upper_chunk(k)
        for d in range(1, reps):
            first_copy(k, d).start()
        return carry

    lax.fori_loop(0, chunks, upper_body, 0)
    for k in range(chunks):
        forward(k)
    for k in range(chunks):
        for s in range(5):
            second_copy(k, s).wait_recv()

    depth = chunks * reps * 16
    own_lanes = iota((depth, LANES), 1) < 32

    def merged(s):
        return jnp.where(
            own_lanes,
            gathered[s].reshape(depth, LANES).astype(F32),
            gathered[s + 1].reshape(depth, LANES).astype(F32),
        )

    mine = merged(0)
    cubes = mine.reshape(chunks * reps, 2, 8, LANES)
    swapped = jnp.concatenate([cubes[:, 1:2], -cubes[:, 0:1]], axis=1).reshape(depth, LANES)
    left = jnp.concatenate([mine.T, swapped.T], axis=0).astype(BF16)
    same_bin = lax.rem(iota((LANES, LANES), 0), GROUP) == lax.rem(iota((LANES, LANES), 1), GROUP)
    pick_row, pick_lane = iota((LANES, LANES), 0), iota((LANES, LANES), 1)
    pick_real = jnp.where(pick_lane == pick_row // GROUP, 1.0, 0.0).astype(BF16)
    pick_imag = jnp.where(pick_lane == 16 + pick_row // GROUP, 1.0, 0.0).astype(BF16)
    picks = jnp.concatenate([pick_real, pick_imag] * 3, axis=0)
    scale = 1.0 / (windows * reps)
    for s in range(5):
        block = (mine if s == 0 else merged(s)).astype(BF16)
        product = dot(left, block)
        real = jnp.where(same_bin, product[0:LANES], 0.0) * scale
        imag = jnp.where(same_bin, product[LANES:], 0.0) * scale
        terms = []
        for _ in range(3):
            real_part, imag_part = real.astype(BF16), imag.astype(BF16)
            terms += [real_part, imag_part]
            real, imag = real - real_part.astype(F32), imag - imag_part.astype(F32)
        tile = dot(jnp.concatenate(terms, axis=1), picks)
        for c in range(16):
            out[c, s] = tile[c * GROUP : (c + 1) * GROUP, 0:32]

    for k in range(chunks):
        rim_copy(k).wait_send()
        for d in range(1, reps):
            first_copy(k, d).wait_send()
        for s in range(5):
            second_copy(k, s).wait_send()
    hist_own.wait_send()
    hist_rim.wait_send()


def solution(mesh):
    chans, reps = mesh.shape["chan"], mesh.shape["rep"]

    def per_device(strain, fir_taps, spatial):
        rows, samples = strain.shape
        windows = samples // NFFT
        chunks = windows // CW
        anywhere = pl.BlockSpec(memory_space=pl.ANY)
        return pl.pallas_call(
            functools.partial(kernel, chans, reps),
            out_shape=jax.ShapeDtypeStruct((rows, 5, BINS // reps, 32), F32),
            in_specs=[anywhere] * 4,
            out_specs=pl.BlockSpec(memory_space=pltpu.VMEM),
            scratch_shapes=[
                pltpu.VMEM((1, fir_taps.shape[0]), F32),
                pltpu.SMEM(spatial.shape, F32),
                pltpu.VMEM((rows, samples + LANES), BF16),
                pltpu.VMEM((8, samples + LANES), BF16),
                pltpu.VMEM((2 * LANES, 2 * LANES), BF16),
                pltpu.VMEM((NFFT + LANES, 2 * LANES), BF16),
                pltpu.VMEM((2 * LANES + 2 * BINS, 1024), BF16),
                pltpu.VMEM((windows, 192, LANES), F32),
                pltpu.VMEM((CW, 32, LANES), F32),
                pltpu.VMEM((windows, 8, LANES), F32),
                pltpu.VMEM((chunks, CW * 16, LANES), F32),
                pltpu.VMEM((chunks, reps, 16, LANES), BF16),
                pltpu.VMEM((6, chunks, reps, 16, LANES), BF16),
                pltpu.VMEM((8, LANES), F32),
                pltpu.SemaphoreType.DMA((4,)),
                pltpu.SemaphoreType.DMA((chunks,)),
                pltpu.SemaphoreType.DMA((chunks,)),
                pltpu.SemaphoreType.DMA((2,)),
                pltpu.SemaphoreType.DMA((2,)),
                pltpu.SemaphoreType.DMA((chunks, 3)),
                pltpu.SemaphoreType.DMA((chunks, 3)),
                pltpu.SemaphoreType.DMA((chunks, 5)),
                pltpu.SemaphoreType.DMA((chunks, 5)),
            ],
            compiler_params=pltpu.CompilerParams(
                collective_id=0, has_side_effects=True, vmem_limit_bytes=67043328
            ),
        )(strain, fir_taps.reshape(1, -1), spatial, jnp.asarray(tables()))

    return jax.shard_map(
        per_device,
        mesh=mesh,
        in_specs=(P("chan", "rep"), P(), P()),
        out_specs=P("chan", None, "rep", None),
        check_vma=False,
    )
```
